32 devices in a mesh: dp: 4 (over z), tensor: 8 (over y, x, core).
Axes of the slice: x: 2, y: 2, z: 4, core: 2. Of those that a mesh axis runs over, the one named last changes fastest.
Arguments:
- block_input: float32 [32, 729, 1152], P(('dp', 'tensor')), may hold values from -6 to 6
- cotangent: bfloat16 [32, 729, 1152], P(('dp', 'tensor')), may hold values from -6 to 6
- w_qkv: bfloat16 [3, 1152, 1152], P(None, None, 'tensor'), may hold values from -1.5 to 1.5
- b_qv: float32 [2, 1152], P(None, 'tensor'), may hold values from -3 to 3
- w_out: bfloat16 [1152, 1152], P('tensor'), may hold values from -3 to 3
- b_out: float32 [1152], replicated, may hold values from -3 to 3
- w_up: bfloat16 [1152, 4304], P(None, 'tensor'), may hold values from -0.1875 to 0.1875
- b_up: float32 [4304], P('tensor'), may hold values from -3 to 3
- w_down: bfloat16 [4304, 1152], P('tensor'), may hold values from -0.09375 to 0.09375
- b_down: float32 [1152], replicated, may hold values from -3 to 3
- ln1_gain: float32 [1152], replicated, may hold values from 0.5 to 1.5
- ln1_shift: float32 [1152], replicated, may hold values from -2 to 2
- ln2_gain: float32 [1152], replicated, may hold values from 0.5 to 1.5
- ln2_shift: float32 [1152], replicated, may hold values from -2 to 2
Outputs:
- block_output: float32 [32, 729, 1152], P(('dp', 'tensor'))
- grad_input: float32 [32, 729, 1152], P(('dp', 'tensor'))
- d_w_qkv: float32 [3, 1152, 1152], P(None, None, 'tensor')
- d_b_qv: float32 [2, 1152], P(None, 'tensor')
- d_w_out: float32 [1152, 1152], P('tensor')
- d_b_out: float32 [1152], replicated
- d_w_up: float32 [1152, 4304], P(None, 'tensor')
- d_b_up: float32 [4304], P('tensor')
- d_w_down: float32 [4304, 1152], P('tensor')
- d_b_down: float32 [1152], replicated
- d_ln1_gain: float32 [1152], replicated
- d_ln1_shift: float32 [1152], replicated
- d_ln2_gain: float32 [1152], replicated
- d_ln2_shift: float32 [1152], replicated
The draws below stay inside these ranges and needn't reach their ends.
All inputs are finite; a program needn't handle non-finite values.
Results may differ from the reference program's by a relative error of at most 0.015.
Values may be sent and summed in bfloat16 or wider, within the bound.
No kernel may reach another device: no remote copies, remote signals or barrier semaphores. Data moves between devices by JAX's collectives and lax.ppermute only.
A program may use at most 768 MiB of HBM per device.

```python
import math
import jax
import jax.numpy as jnp
from jax import lax

D = 1152
HEADS = 16
HD = 72
FF = 4304
SEQ = 729
IMAGES = 32


def draw_w_qkv(key, part):
    first_key = jax.random.fold_in(jax.random.fold_in(key, 17), 0)
    noise_draw = jax.random.normal(first_key, (3, D, HEADS * HD), jnp.float32)
    drawn_vals = noise_draw / math.sqrt(D)
    return jnp.clip(drawn_vals, -1.5, 1.5).astype(jnp.bfloat16)


def level_of(key, shape, pieces, least, top_value):
    loudness, own = 1.0, jax.random.fold_in(key, 6)
    for position, shards_of in pieces:
        draws = jnp.exp(jax.random.uniform(jax.random.fold_in(own, position), (shards_of,), jnp.float32, least / len(pieces), top_value / len(pieces)))
        loudness = loudness * jnp.repeat(draws, shape[position] // shards_of).reshape([-1 if axis == position else 1 for axis in range(len(shape))])
    return loudness


def bell_draw(own_key, shape, deviation, most, cuts=(), dtype=jnp.bfloat16):
    entries = deviation * jax.random.normal(own_key, shape, jnp.float32)
    if cuts:
        entries = entries * level_of(own_key, shape, cuts, -0.22, 0.18)
    return jnp.clip(entries, -most, most).astype(dtype)


def setup_inputs(seed: int = 0) -> dict:
    streams_of = jax.random.split(jax.random.key(seed), 15)
    block_input = bell_draw(streams_of[0], (IMAGES, SEQ, D), 1.0, 6.0, ((0, 32),), jnp.float32)
    cotangent = bell_draw(streams_of[1], (IMAGES, SEQ, D), 1.0, 6.0, ((0, 32),))
    w_qkv = draw_w_qkv(jax.random.fold_in(streams_of[14], 71), 0)
    b_qv = bell_draw(streams_of[3], (2, HEADS * HD), 0.5, 3.0, ((1, 8),), jnp.float32)
    w_out = bell_draw(streams_of[4], (HEADS * HD, D), (max(HEADS * HD // 256, 1)) ** -0.5, 3.0, ((0, 8),))
    b_out = bell_draw(streams_of[5], (D,), 0.5, 3.0, (), jnp.float32)
    w_up = bell_draw(streams_of[6], (D, FF), D ** -0.5, 0.1875, ((1, 8),))
    b_up = bell_draw(streams_of[7], (FF,), 0.5, 3.0, ((0, 8),), jnp.float32)
    w_down = bell_draw(streams_of[8], (FF, D), FF ** -0.5, 0.09375, ((0, 8),))
    b_down = bell_draw(streams_of[9], (D,), 0.5, 3.0, (), jnp.float32)
    ln1_gain = jnp.clip(1.0 + 0.1 * jax.random.normal(streams_of[10], (D,), jnp.float32), 0.5, 1.5)
    ln1_shift = bell_draw(streams_of[11], (D,), 0.3, 2.0, (), jnp.float32)
    ln2_gain = jnp.clip(1.0 + 0.1 * jax.random.normal(streams_of[12], (D,), jnp.float32), 0.5, 1.5)
    ln2_shift = bell_draw(streams_of[13], (D,), 0.3, 2.0, (), jnp.float32)
    return {"block_input": block_input, "cotangent": cotangent, "w_qkv": w_qkv, "b_qv": b_qv, "w_out": w_out, "b_out": b_out, "w_up": w_up, "b_up": b_up, "w_down": w_down, "b_down": b_down, "ln1_gain": ln1_gain, "ln1_shift": ln1_shift, "ln2_gain": ln2_gain, "ln2_shift": ln2_shift}


EPS = 1e-06

def dot_nn(left_mat, right_mat):
    return jnp.dot(left_mat, right_mat, preferred_element_type=jnp.float32)

def dot_tn(left_mat, right_mat):
    return lax.dot_general(left_mat, right_mat, (((0,), (0,)), ((), ())), preferred_element_type=jnp.float32)

def dot_nt(left_mat, right_mat):
    return lax.dot_general(left_mat, right_mat, (((1,), (1,)), ((), ())), preferred_element_type=jnp.float32)

def normalize(stream, gain_vec, shift_vec):
    mean_row = lax.optimization_barrier(jnp.mean(stream, axis=-1, keepdims=True))
    centred = stream - mean_row
    variance = lax.optimization_barrier(jnp.mean(centred * centred, axis=-1, keepdims=True))
    inverse = lax.rsqrt(variance + EPS)
    unit_rows = centred * inverse
    return (unit_rows * gain_vec + shift_vec, unit_rows, inverse)

def norm_back(grad_out, unit_rows, inverse, gain_vec):
    scaled = grad_out * gain_vec
    avg_plain = lax.optimization_barrier(jnp.mean(scaled, axis=-1, keepdims=True))
    avg_unit = lax.optimization_barrier(jnp.mean(scaled * unit_rows, axis=-1, keepdims=True))
    return inverse * (scaled - avg_plain - unit_rows * avg_unit)

def gelu_tanh(values_in):
    return jax.nn.gelu(values_in, approximate=True)

def to_items(flat_rows, head_count, seq_len):
    images = flat_rows.shape[0] // seq_len
    head_dim = flat_rows.shape[1] // head_count
    shaped = flat_rows.reshape(images, seq_len, head_count, head_dim).transpose(0, 2, 1, 3)
    return shaped.reshape(images * head_count, seq_len, head_dim)

def from_items(items, head_count, seq_len):
    number, length, head_dim = items.shape
    shaped = items.reshape(number // head_count, head_count, length, head_dim).transpose(0, 2, 1, 3)
    return shaped.reshape(number // head_count * length, head_count * head_dim)

def attend_one(bundle):
    queries, key_rows, values_in = bundle
    score_scale = 1.0 / math.sqrt(queries.shape[-1])
    scores = dot_nt(queries, key_rows) * score_scale
    row_max = lax.optimization_barrier(jnp.max(scores, axis=-1, keepdims=True))
    exp_total = lax.optimization_barrier(jnp.sum(jnp.exp(scores - row_max), axis=-1, keepdims=True))
    logsum = row_max + jnp.log(exp_total)
    probabilities = jnp.exp(scores - logsum).astype(jnp.bfloat16)
    result = dot_nn(probabilities, values_in).astype(jnp.bfloat16)
    return (result, logsum[:, 0])

def attend_back_one(bundle):
    queries, key_rows, values_in, result, grad_out, logsum = bundle
    score_scale = 1.0 / math.sqrt(queries.shape[-1])
    scores = dot_nt(queries, key_rows) * score_scale
    probabilities = jnp.exp(scores - logsum[:, None])
    grad_probs = dot_nt(grad_out, values_in)
    row_dot = lax.optimization_barrier(jnp.sum(grad_out.astype(jnp.float32) * result.astype(jnp.float32), axis=-1, keepdims=True))
    grad_scores = (probabilities * (grad_probs - row_dot) * score_scale).astype(jnp.bfloat16)
    grad_query = dot_nn(grad_scores, key_rows).astype(jnp.bfloat16)
    grad_key = dot_tn(grad_scores, queries).astype(jnp.bfloat16)
    grad_value = dot_tn(probabilities.astype(jnp.bfloat16), grad_out).astype(jnp.bfloat16)
    return (grad_query, grad_key, grad_value)

def reference(block_input, cotangent, w_qkv, b_qv, w_out, b_out, w_up, b_up, w_down, b_down, ln1_gain, ln1_shift, ln2_gain, ln2_shift):
    bf_type = jnp.bfloat16
    fl_type = jnp.float32

    def one_image(grads_acc, bundle):
        stream, grad_y = bundle
        grad_f = grad_y.astype(fl_type)
        normed1, unit_one, inv_one = normalize(stream, ln1_gain, ln1_shift)
        normed1 = normed1.astype(bf_type)
        queries = (dot_nn(normed1, w_qkv[0]) + b_qv[0]).astype(bf_type)
        key_rows = dot_nn(normed1, w_qkv[1]).astype(bf_type)
        values_in = (dot_nn(normed1, w_qkv[2]) + b_qv[1]).astype(bf_type)
        q_items = to_items(queries, HEADS, SEQ)
        k_items = to_items(key_rows, HEADS, SEQ)
        v_items = to_items(values_in, HEADS, SEQ)
        o_items, logsum = lax.map(attend_one, (q_items, k_items, v_items))
        attn_heads = from_items(o_items, HEADS, SEQ)
        hidden_res = stream + dot_nn(attn_heads, w_out) + b_out
        normed2, unit_two, inv_two = normalize(hidden_res, ln2_gain, ln2_shift)
        normed2 = normed2.astype(bf_type)
        pre_act = dot_nn(normed2, w_up) + b_up
        activated, gelu_back = jax.vjp(gelu_tanh, pre_act)
        act_b = activated.astype(bf_type)
        block_output = hidden_res + dot_nn(act_b, w_down) + b_down
        g_down = dot_tn(act_b, grad_y)
        g_downb = lax.optimization_barrier(jnp.sum(grad_f, axis=0))
        grad_pre = gelu_back(dot_nt(grad_y, w_down))[0].astype(bf_type)
        g_up = dot_tn(normed2, grad_pre)
        g_upb = lax.optimization_barrier(jnp.sum(grad_pre.astype(fl_type), axis=0))
        grad_n2 = dot_nt(grad_pre, w_up)
        g2_gain = lax.optimization_barrier(jnp.sum(grad_n2 * unit_two, axis=0))
        g2_shift = lax.optimization_barrier(jnp.sum(grad_n2, axis=0))
        grad_hid = grad_f + norm_back(grad_n2, unit_two, inv_two, ln2_gain)
        grad_hid_b = grad_hid.astype(bf_type)
        g_outb = lax.optimization_barrier(jnp.sum(grad_hid, axis=0))
        g_out = dot_tn(attn_heads, grad_hid_b)
        grad_heads = dot_nt(grad_hid_b, w_out).astype(bf_type)
        gh_items = to_items(grad_heads, HEADS, SEQ)
        gq_items, gk_items, gv_items = lax.map(attend_back_one, (q_items, k_items, v_items, o_items, gh_items, logsum))
        grad_q = from_items(gq_items, HEADS, SEQ)
        grad_k = from_items(gk_items, HEADS, SEQ)
        grad_v = from_items(gv_items, HEADS, SEQ)
        g_qkv = jnp.stack([dot_tn(normed1, grad_q), dot_tn(normed1, grad_k), dot_tn(normed1, grad_v)])
        g_qvb = jnp.stack([lax.optimization_barrier(jnp.sum(grad_q.astype(fl_type), axis=0)), lax.optimization_barrier(jnp.sum(grad_v.astype(fl_type), axis=0))])
        grad_n1 = dot_nt(grad_q, w_qkv[0]) + dot_nt(grad_k, w_qkv[1]) + dot_nt(grad_v, w_qkv[2])
        g1_gain = lax.optimization_barrier(jnp.sum(grad_n1 * unit_one, axis=0))
        g1_shift = lax.optimization_barrier(jnp.sum(grad_n1, axis=0))
        grad_in = grad_hid + norm_back(grad_n1, unit_one, inv_one, ln1_gain)
        terms = (g_qkv, g_qvb, g_out, g_outb, g_up, g_upb, g_down, g_downb, g1_gain, g1_shift, g2_gain, g2_shift)
        grads_acc = tuple((acc_term + new_term for acc_term, new_term in zip(grads_acc, terms)))
        return (grads_acc, (block_output, grad_in))
    start_grads = (jnp.zeros((3, D, HEADS * HD), fl_type), jnp.zeros((2, HEADS * HD), fl_type), jnp.zeros((HEADS * HD, D), fl_type), jnp.zeros((D,), fl_type), jnp.zeros((D, FF), fl_type), jnp.zeros((FF,), fl_type), jnp.zeros((FF, D), fl_type), jnp.zeros((D,), fl_type), jnp.zeros((D,), fl_type), jnp.zeros((D,), fl_type), jnp.zeros((D,), fl_type), jnp.zeros((D,), fl_type))
    grads_acc, (outputs, grads_in) = lax.scan(one_image, start_grads, (block_input, cotangent))
    g_qkv, g_qvb, g_out, g_outb, g_up, g_upb, g_down, g_downb, g1_gain, g1_shift, g2_gain, g2_shift = grads_acc
    return (outputs, grads_in, g_qkv, g_qvb, g_out, g_outb, g_up, g_upb, g_down, g_downb, g1_gain, g1_shift, g2_gain, g2_shift)
```

```python
import functools
import math

import jax
import jax.numpy as jnp
from jax import lax
from jax.experimental import pallas as pl
from jax.experimental.pallas import tpu as pltpu
from jax.sharding import PartitionSpec as P

HD = 72
EPS = 1e-06
LOG2E = 1.4426950408889634
ROW_TILE = 16
VMEM_BYTES = 60 << 20

bf_type = jnp.bfloat16
fl_type = jnp.float32


def dot(left_mat, right_mat, left_dim, right_dim):
    return lax.dot_general(
        left_mat,
        right_mat,
        (((left_dim,), (right_dim,)), ((), ())),
        preferred_element_type=jnp.float32,
    )


def in_vmem():
    return pl.BlockSpec(memory_space=pltpu.VMEM)


def attend_kernel(q_ref, k_ref, v_ref, o_ref, lse_ref, qs, ks, vs, *, heads):
    for h in range(heads):
        cols = slice(h * HD, (h + 1) * HD)
        qs[h] = q_ref[:, cols]
        ks[h] = k_ref[:, cols]
        vs[h] = v_ref[:, cols]
    scale = 1.0 / math.sqrt(HD)

    def body(h, carry):
        scores = dot(ks[h], qs[h], 1, 1)
        top = jnp.max(scores, axis=0, keepdims=True)
        powers = jnp.exp2((scores - top) * (scale * LOG2E))
        total = jnp.sum(powers, axis=0, keepdims=True)
        out = dot(vs[h], powers.astype(bf_type), 0, 0) * (1.0 / total)
        qs[h] = out.T.astype(bf_type)
        lse_ref[h] = top * scale + jnp.log(total)
        return carry

    lax.fori_loop(0, heads, body, 0, unroll=2)
    for h in range(heads):
        o_ref[:, h * HD : (h + 1) * HD] = qs[h]


def attend(queries, key_rows, values_in):
    rows, width = queries.shape
    heads = width // HD
    return pl.pallas_call(
        functools.partial(attend_kernel, heads=heads),
        out_shape=(
            jax.ShapeDtypeStruct((rows, width), bf_type),
            jax.ShapeDtypeStruct((heads, 1, rows), fl_type),
        ),
        in_specs=[in_vmem()] * 3,
        out_specs=(in_vmem(), in_vmem()),
        scratch_shapes=[pltpu.VMEM((heads, rows, HD), bf_type)] * 3,
        compiler_params=pltpu.CompilerParams(vmem_limit_bytes=VMEM_BYTES),
        cost_estimate=pl.CostEstimate(
            flops=16 * rows * rows * width,
            bytes_accessed=8 * rows * width,
            transcendentals=heads * rows * rows,
        ),
        name="attend",
    )(queries, key_rows, values_in)


def attend_back_kernel(
    q_ref, k_ref, v_ref, o_ref, g_ref, lse_ref, dq_ref, dk_ref, dv_ref, qs, ks, vs, os, gs, *, heads
):
    for h in range(heads):
        cols = slice(h * HD, (h + 1) * HD)
        qs[h] = q_ref[:, cols]
        ks[h] = k_ref[:, cols]
        vs[h] = v_ref[:, cols]
        os[h] = o_ref[:, cols]
        gs[h] = g_ref[:, cols]
    scale = 1.0 / math.sqrt(HD)

    def body(h, carry):
        queries, key_rows, values_in, grad_out = qs[h], ks[h], vs[h], gs[h]
        scores = dot(key_rows, queries, 1, 1)
        probs = jnp.exp2(scores * (scale * LOG2E) - lse_ref[h] * LOG2E)
        grad_probs = dot(values_in, grad_out, 1, 1)
        row_dot = jnp.sum(
            (grad_out.astype(fl_type) * os[h].astype(fl_type)).T, axis=0, keepdims=True
        )
        grad_scores = (probs * (grad_probs - row_dot)).astype(bf_type)
        grad_value = dot(probs.astype(bf_type), grad_out, 1, 0)
        grad_key = dot(grad_scores, queries, 1, 0) * scale
        grad_query = dot(key_rows, grad_scores, 0, 0) * scale
        vs[h] = grad_value.astype(bf_type)
        ks[h] = grad_key.astype(bf_type)
        qs[h] = grad_query.T.astype(bf_type)
        return carry

    lax.fori_loop(0, heads, body, 0, unroll=2)
    for h in range(heads):
        cols = slice(h * HD, (h + 1) * HD)
        dq_ref[:, cols] = qs[h]
        dk_ref[:, cols] = ks[h]
        dv_ref[:, cols] = vs[h]


def attend_back(queries, key_rows, values_in, out, grad_out, logsum):
    rows, width = queries.shape
    heads = width // HD
    return pl.pallas_call(
        functools.partial(attend_back_kernel, heads=heads),
        out_shape=(jax.ShapeDtypeStruct((rows, width), bf_type),) * 3,
        in_specs=[in_vmem()] * 6,
        out_specs=(in_vmem(),) * 3,
        scratch_shapes=[pltpu.VMEM((heads, rows, HD), bf_type)] * 5,
        compiler_params=pltpu.CompilerParams(vmem_limit_bytes=VMEM_BYTES),
        cost_estimate=pl.CostEstimate(
            flops=30 * rows * rows * width,
            bytes_accessed=16 * rows * width,
            transcendentals=heads * rows * rows,
        ),
        name="attend_back",
    )(queries, key_rows, values_in, out, grad_out, logsum)


def pair_grad_kernel(left_ref, right_ref, left2_ref, right2_ref, out_ref):
    out_ref[...] = (
        dot(left_ref[...], right_ref[...], 0, 0) + dot(left2_ref[...], right2_ref[...], 0, 0)
    ).astype(out_ref.dtype)


def split_of(total, most):
    sizes = [s for s in range(128, most + 1, 128) if total % s == 0]
    return sizes[-1] if sizes else total


def pair_grad(left, right, left2, right2, most=1152):
    rows, width = left.shape
    columns = right.shape[1]
    size = split_of(width, most)
    return pl.pallas_call(
        pair_grad_kernel,
        grid=(width // size,),
        out_shape=jax.ShapeDtypeStruct((width, columns), bf_type),
        in_specs=[
            pl.BlockSpec((rows, size), lambda i: (0, i)),
            pl.BlockSpec((rows, columns), lambda i: (0, 0)),
            pl.BlockSpec((rows, size), lambda i: (0, i)),
            pl.BlockSpec((rows, columns), lambda i: (0, 0)),
        ],
        out_specs=pl.BlockSpec((size, columns), lambda i: (i, 0)),
        compiler_params=pltpu.CompilerParams(vmem_limit_bytes=VMEM_BYTES),
        cost_estimate=pl.CostEstimate(
            flops=4 * rows * width * columns,
            bytes_accessed=4 * rows * (width + columns) + 2 * width * columns,
            transcendentals=0,
        ),
        name="pair_grad",
    )(left, right, left2, right2)


def normalize(stream, gain_vec, shift_vec):
    mean_row = jnp.mean(stream, axis=-1, keepdims=True)
    centred = stream - mean_row
    variance = jnp.mean(centred * centred, axis=-1, keepdims=True)
    inverse = lax.rsqrt(variance + EPS)
    unit_rows = centred * inverse
    return (unit_rows * gain_vec + shift_vec, unit_rows, inverse)


def norm_back(grad_out, unit_rows, inverse, gain_vec):
    scaled = grad_out * gain_vec
    avg_plain = jnp.mean(scaled, axis=-1, keepdims=True)
    avg_unit = jnp.mean(scaled * unit_rows, axis=-1, keepdims=True)
    return inverse * (scaled - avg_plain - unit_rows * avg_unit)


def swap(value, axis, bit):
    count = lax.axis_size(axis)
    return lax.ppermute(value, axis, [(i, i ^ bit) for i in range(count)])


def far_bits(group):
    return [1 << k for k in range(1, group.bit_length() - 1)]


def piece_order(group):
    return list(range(0, group, 2)) + list(range(1, group, 2))


def gather_pieces(shard, group, flip):
    bits = far_bits(group)
    if flip:
        bits = bits[::-1]
    pieces = {0: shard}
    for bit in bits:
        for i in list(pieces):
            pieces[i ^ bit] = swap(pieces[i], "tensor", bit)
    for i in list(pieces):
        pieces[i ^ 1] = swap(pieces[i], "tensor", 1)
    return pieces


def scatter_sum(blocks, group, flip):
    bits = far_bits(group)
    if flip:
        bits = bits[::-1]
    for bit in bits:
        sent = sorted(i for i in blocks if i & bit)
        rows = blocks[sent[0]].shape[0]
        joined = jnp.concatenate([blocks[i] for i in sent], axis=0)
        came = swap(joined, "tensor", bit)
        kept = {}
        for place, i in enumerate(sent):
            part = came[place * rows : (place + 1) * rows]
            kept[i ^ bit] = (blocks[i ^ bit].astype(fl_type) + part.astype(fl_type)).astype(bf_type)
        blocks = kept
    return blocks[0]


def sum_over_dp(value):
    count = lax.axis_size("dp")
    if count == 1:
        return value
    half = value.shape[0] // 2
    odd = (lax.axis_index("dp") & 1) == 1
    low, high = value[:half], value[half:]
    mine = jnp.where(odd, high, low).astype(fl_type)
    came = swap(jnp.where(odd, low, high), "dp", 1)
    mine = (mine + came.astype(fl_type)).astype(bf_type)
    bit = 2
    while bit < count:
        came = swap(mine, "dp", bit)
        mine = (mine.astype(fl_type) + came.astype(fl_type)).astype(bf_type)
        bit *= 2
    other = swap(mine, "dp", 1)
    return jnp.concatenate([jnp.where(odd, other, mine), jnp.where(odd, mine, other)], axis=0)


def sum_small(owned, shared, group):
    n = owned.shape[1]
    joined = jnp.concatenate([owned, shared], axis=1)
    bit = 1
    while bit < group:
        came = swap(joined, "tensor", bit)
        order = [i ^ bit for i in range(group)]
        came_owned = jnp.concatenate([came[i : i + 1, :n] for i in order], axis=0)
        joined = joined + jnp.concatenate([came_owned, came[:, n:]], axis=1)
        bit *= 2
    joined = jnp.concatenate(
        [jnp.broadcast_to(joined[:1, :n], (group, n)), joined[:, n:]], axis=1
    )
    bit = 1
    while bit < lax.axis_size("dp"):
        joined = joined + swap(joined, "dp", bit)
        bit *= 2
    return joined[0, :n], joined[:, n:]


def per_device(
    block_input,
    cotangent,
    w_qkv,
    b_qv,
    w_out,
    b_out,
    w_up,
    b_up,
    w_down,
    b_down,
    ln1_gain,
    ln1_shift,
    ln2_gain,
    ln2_shift,
):
    images, seq_len, feature_dim = block_input.shape
    row_count = images * seq_len
    group = lax.axis_size("tensor")
    me = lax.axis_index("tensor")
    order = piece_order(group)
    half_group = group // 2
    stream = block_input.reshape(row_count, feature_dim)
    grad_y = cotangent.reshape(row_count, feature_dim)
    grad_f = grad_y.astype(fl_type)
    head_cols = w_qkv.shape[2]
    hidden_cols = w_up.shape[1]
    hidden_pad = -(-hidden_cols // ROW_TILE) * ROW_TILE
    extra = hidden_pad - hidden_cols

    first = jnp.concatenate(
        [w_qkv.transpose(0, 2, 1).reshape(3 * head_cols, feature_dim), w_out], axis=0
    )
    up_rows = jnp.pad(w_up.T, ((0, extra), (0, 0)))
    down_rows = jnp.pad(w_down, ((0, extra), (0, 0)))
    biases = jnp.concatenate([b_qv.reshape(-1), jnp.pad(b_up, (0, extra))])
    bias_all = lax.all_gather(biases, "tensor", axis=0)
    bias_all = jnp.concatenate(
        [lax.dynamic_slice_in_dim(bias_all, me ^ i, 1, axis=0) for i in order], axis=0
    )
    bias_q = bias_all[:, :head_cols].reshape(-1)
    bias_v = bias_all[:, head_cols : 2 * head_cols].reshape(-1)
    bias_up = bias_all[:, 2 * head_cols :].reshape(-1)

    first_pieces = gather_pieces(first, group, False)
    up_pieces = gather_pieces(up_rows, group, True)
    down_pieces = gather_pieces(down_rows, group, False)

    def joined(pieces, start, stop, which=order):
        return jnp.concatenate([pieces[i][start:stop] for i in which], axis=0)

    q_w = joined(first_pieces, 0, head_cols)
    k_w = joined(first_pieces, head_cols, 2 * head_cols)
    v_w = joined(first_pieces, 2 * head_cols, 3 * head_cols)
    o_w = joined(first_pieces, 3 * head_cols, 4 * head_cols)
    u_w = joined(up_pieces, 0, hidden_pad)
    d_w = joined(down_pieces, 0, hidden_pad)

    grad_y2 = swap(grad_y, "tensor", 1)

    normed1, unit_one, inv_one = normalize(stream, ln1_gain, ln1_shift)
    normed1 = normed1.astype(bf_type)
    queries = (dot(normed1, q_w, 1, 1) + bias_q).astype(bf_type)
    key_rows = dot(normed1, k_w, 1, 1).astype(bf_type)
    values_in = (dot(normed1, v_w, 1, 1) + bias_v).astype(bf_type)
    attn_heads, logsum = attend(queries, key_rows, values_in)
    hidden_res = stream + dot(attn_heads, o_w, 1, 0) + b_out
    normed2, unit_two, inv_two = normalize(hidden_res, ln2_gain, ln2_shift)
    normed2 = normed2.astype(bf_type)
    pre_act = dot(normed2, u_w, 1, 1) + bias_up
    activated, gelu_back = jax.vjp(lambda v: jax.nn.gelu(v, approximate=True), pre_act)
    act_b = activated.astype(bf_type)
    block_output = hidden_res + dot(act_b, d_w, 1, 0) + b_down

    def halves(value):
        middle = value.shape[1] // 2
        return value[:, :middle], value[:, middle:]

    def weight_sum(value, right, right2, flip):
        kept, sent = halves(value)
        came = swap(sent, "tensor", 1)
        grads = pair_grad(kept, right, came, right2)
        rows = grads.shape[0] // half_group
        blocks = {i: grads[(i // 2) * rows : (i // 2 + 1) * rows] for i in range(0, group, 2)}
        total = scatter_sum(blocks, group, flip)
        return sum_over_dp(total)

    g_down = weight_sum(act_b, grad_y, grad_y2, False)
    g_downb = jnp.sum(grad_f, axis=0)
    grad_pre = gelu_back(dot(grad_y, d_w, 1, 1))[0].astype(bf_type)
    g_upb = jnp.sum(grad_pre.astype(fl_type), axis=0)
    grad_n2 = dot(grad_pre, u_w, 1, 0)
    normed2_2 = swap(normed2, "tensor", 1)
    g_up = weight_sum(grad_pre, normed2, normed2_2, True)
    g2_gain = jnp.sum(grad_n2 * unit_two, axis=0)
    g2_shift = jnp.sum(grad_n2, axis=0)
    grad_hid = grad_f + norm_back(grad_n2, unit_two, inv_two, ln2_gain)
    grad_hid_b = grad_hid.astype(bf_type)
    g_outb = jnp.sum(grad_hid, axis=0)
    grad_heads = dot(grad_hid_b, o_w, 1, 1).astype(bf_type)
    g_out = weight_sum(attn_heads, grad_hid_b, swap(grad_hid_b, "tensor", 1), False)
    grad_q, grad_k, grad_v = attend_back(
        queries, key_rows, values_in, attn_heads, grad_heads, logsum
    )
    normed1_2 = swap(normed1, "tensor", 1)
    g_q = weight_sum(grad_q, normed1, normed1_2, False)
    g_k = weight_sum(grad_k, normed1, normed1_2, True)
    g_v = weight_sum(grad_v, normed1, normed1_2, False)
    grad_n1 = dot(grad_q, q_w, 1, 0) + dot(grad_k, k_w, 1, 0) + dot(grad_v, v_w, 1, 0)
    g1_gain = jnp.sum(grad_n1 * unit_one, axis=0)
    g1_shift = jnp.sum(grad_n1, axis=0)
    grad_in = grad_hid + norm_back(grad_n1, unit_one, inv_one, ln1_gain)

    def by_piece(vector):
        rows = vector.reshape(group, -1)
        back = [order.index(i) for i in range(group)]
        return jnp.concatenate([rows[b : b + 1] for b in back], axis=0)

    g_qb = jnp.sum(grad_q.astype(fl_type), axis=0)
    g_vb = jnp.sum(grad_v.astype(fl_type), axis=0)
    owned = jnp.concatenate([by_piece(g_qb), by_piece(g_vb), by_piece(g_upb)], axis=1)
    shared = jnp.stack([g_outb, g_downb, g1_gain, g1_shift, g2_gain, g2_shift])
    own_sum, shared_sum = sum_small(owned, shared.reshape(group, -1), group)
    shared_sum = shared_sum.reshape(6, feature_dim)
    g_qvb = own_sum[: 2 * head_cols].reshape(2, head_cols)
    g_upb = own_sum[2 * head_cols : 2 * head_cols + hidden_cols]
    g_qkv = jnp.stack([g_q.T, g_k.T, g_v.T]).astype(fl_type)
    return (
        block_output.reshape(images, seq_len, feature_dim),
        grad_in.reshape(images, seq_len, feature_dim),
        g_qkv,
        g_qvb,
        g_out.astype(fl_type),
        shared_sum[0],
        g_up[:hidden_cols].T.astype(fl_type),
        g_upb,
        g_down[:hidden_cols].astype(fl_type),
        shared_sum[1],
        shared_sum[2],
        shared_sum[3],
        shared_sum[4],
        shared_sum[5],
    )


def solution(mesh):
    in_specs = (
        P(("dp", "tensor"), None, None),
        P(("dp", "tensor"), None, None),
        P(None, None, "tensor"),
        P(None, "tensor"),
        P("tensor", None),
        P(),
        P(None, "tensor"),
        P("tensor"),
        P("tensor", None),
        P(),
        P(),
        P(),
        P(),
        P(),
    )
    out_specs = (
        P(("dp", "tensor"), None, None),
        P(("dp", "tensor"), None, None),
        P(None, None, "tensor"),
        P(None, "tensor"),
        P("tensor", None),
        P(),
        P(None, "tensor"),
        P("tensor"),
        P("tensor", None),
        P(),
        P(),
        P(),
        P(),
        P(),
    )
    return jax.shard_map(
        per_device, mesh=mesh, in_specs=in_specs, out_specs=out_specs, check_vma=False
    )
```
